256 devices in a mesh: space: 16 (over x_hi, z), chan: 16 (over y, x_lo, core).
Axes of the slice: x: 4 (x_hi: 2, x_lo: 2; x = x_hi * 2 + x_lo), y: 4, z: 8, core: 2. Of those that a mesh axis runs over, the one named last changes fastest.
Arguments:
- activations: bfloat16 [512, 128, 16, 128], P('chan', 'space'), may hold values from -6 to 6
- out_grad: bfloat16 [512, 128, 16, 128], P('chan', 'space'), may hold values from -6 to 6
Outputs:
- filter_grad: float32 [27, 512, 512], P(None, 'space', 'chan')
The draws below stay inside these ranges and needn't reach their ends.
All inputs are finite; a program needn't handle non-finite values.
Results may differ from the reference program's by a relative error of at most 0.0003.
Values may be sent and summed in bfloat16 or wider, within the bound.
No kernel may reach another device: no remote copies, remote signals or barrier semaphores. Data moves between devices by JAX's collectives and lax.ppermute only.
A program may use at most 192 MiB of HBM per device.

```python
import jax
import jax.numpy as jnp
from jax import lax

CIN = 512
COUT = 512
NY = 16
NZ = 128
NX = 128


def with_spikes(result, key, source, target, blocks, factor):
    owner, partner = [(jnp.arange(result.shape[axis_at]) // (result.shape[axis_at] // blocks)).reshape([-1 if axis == axis_at else 1 for axis in range(result.ndim)]) for axis_at in (source, target)]
    chosen = jax.random.permutation(key, blocks)[partner]
    strong = (owner == chosen) | (owner == (partner + blocks // 2) % blocks)
    return jnp.where(strong, factor * result, result)


def shard_levels(key, shape, cuts, smallest, largest):
    def one(axis_at, blocks):
        draws = jax.random.uniform(jax.random.fold_in(jax.random.fold_in(key, 6), axis_at), (blocks,), jnp.float32, smallest / len(cuts), largest / len(cuts))
        return jnp.repeat(jnp.exp(draws), shape[axis_at] // blocks).reshape((-1,) + (1,) * (len(shape) - axis_at - 1))

    gain = one(*cuts[0])
    for cut in cuts[1:]:
        gain = gain * one(*cut)
    return gain


def bell_draw(stream_key, shape, deviation, reach, cuts=(), dtype=jnp.bfloat16):
    factor_of = shard_levels(stream_key, shape, cuts, -0.22, 0.18) if cuts else 1.0
    result = jax.random.normal(stream_key, shape, jnp.float32) * deviation * factor_of
    return jnp.minimum(jnp.maximum(result, -reach), reach).astype(dtype)


def gaussian_with(stream_key, extent, deviation, reach, pieces, heavy, dtype=jnp.bfloat16):
    drawn = deviation * jax.random.normal(stream_key, extent, jnp.float32)
    if pieces:
        drawn = drawn * shard_levels(stream_key, extent, pieces, -0.22, 0.18)
    return jnp.clip(with_spikes(drawn, jax.random.fold_in(stream_key, 3), *heavy), -reach, reach).astype(dtype)


def setup_inputs(seed: int = 0) -> dict:
    seeds = jax.random.split(jax.random.key(seed), 3)
    activations = bell_draw(seeds[0], (CIN, NX, NY, NZ), 1.0, 6.0, ((0, 16), (1, 16)))
    out_grad = gaussian_with(seeds[1], (COUT, NX, NY, NZ), 1.0, 6.0, ((0, 16), (1, 16)), (1, 0, 16, 2.0))
    return {"activations": activations, "out_grad": out_grad}


def reference(activations, out_grad):
    padded = jnp.pad(activations, ((0, 0), (1, 1), (1, 1), (1, 1)))
    flat_grad = out_grad.reshape(COUT, NX * NY * NZ)
    results = []
    for shift_a in range(3):
        for shift_b in range(3):
            for shift_c in range(3):
                window = padded[:, shift_a:shift_a + NX, shift_b:shift_b + NY, shift_c:shift_c + NZ]
                window = window.reshape(CIN, NX * NY * NZ)
                results.append(lax.dot_general(flat_grad, window, (((1,), (1,)), ((), ())), preferred_element_type=jnp.float32))
    scale = jnp.float32(1.0) / jnp.sqrt(jnp.float32(NX * NY * NZ))
    return jnp.stack(results) * scale
```

```python
import functools

import jax
import jax.numpy as jnp
from jax import lax
from jax.experimental import pallas as pl
from jax.experimental.pallas import tpu as pltpu
from jax.sharding import PartitionSpec as P


AXES = ("space", "chan")
SIZES = (("h", 2), ("z", 8), ("y", 4), ("x", 2), ("k", 2))


def place(index):
    found = {}
    for name, size in reversed(SIZES):
        index, found[name] = divmod(index, size)
    return found


def index_of(found):
    index = 0
    for name, size in SIZES:
        index = index * size + found[name] % size
    return index


def send(value, move):
    pairs = [(i, index_of(move(place(i)))) for i in range(256)]
    return lax.ppermute(value, AXES, pairs)


def shift(value, **steps):
    return send(value, lambda d: {n: d[n] + steps.get(n, 0) for n in d})


def halo_pairs(step):
    count = lax.axis_size("space")
    return [(i, i + step) for i in range(count) if 0 <= i + step < count]


def windows_body(size_z, in_ref, out_ref):
    rows, lanes = in_ref.shape
    center = in_ref[...].astype(jnp.float32)
    z = lax.broadcasted_iota(jnp.int32, center.shape, 1) % size_z
    below = jnp.where(z == 0, 0.0, pltpu.roll(center, 1, 1))
    above = jnp.where(z == size_z - 1, 0.0, pltpu.roll(center, lanes - 1, 1))
    blank = jnp.zeros((rows, size_z), out_ref.dtype)
    for c, value in enumerate((below, center, above)):
        value = value.astype(out_ref.dtype)
        for b in range(3):
            at = pl.ds((3 * b + c) * rows, rows)
            if b == 0:
                out_ref[at, :size_z] = blank
                out_ref[at, size_z:] = value[:, : lanes - size_z]
            elif b == 1:
                out_ref[at, :] = value
            else:
                out_ref[at, : lanes - size_z] = value[:, size_z:]
                out_ref[at, lanes - size_z :] = blank


def windows_of(padded, size_z, lanes):
    rows, total = padded.shape
    return pl.pallas_call(
        functools.partial(windows_body, size_z),
        grid=(total // lanes,),
        in_specs=[pl.BlockSpec((rows, lanes), lambda x: (0, x))],
        out_specs=pl.BlockSpec((9 * rows, lanes), lambda x: (0, x)),
        out_shape=jax.ShapeDtypeStruct((9 * rows, total), padded.dtype),
        cost_estimate=pl.CostEstimate(flops=0, bytes_accessed=20 * rows * total, transcendentals=0),
    )(padded)


def pack_body(x_ref, t_ref, out_ref):
    lane = lax.broadcasted_iota(jnp.int32, (9, 8, 128), 2) // 32
    for h in range(2):
        rows = [t_ref[0, :, 0, q, :, h * 128 : (h + 1) * 128] for q in range(4)]
        for group in range(4):
            b, c = divmod(group, 2)
            value = None
            for q in range(4):
                turn = (q - group) % 4 * 32
                moved = rows[q].reshape(72, 128)
                if turn:
                    moved = pltpu.roll(moved, turn, 1)
                moved = moved.reshape(9, 8, 128)
                value = moved if value is None else jnp.where(lane == q, moved, value)
            out_ref[b, 0, c, h] = value


def pack(parts, x):
    grid_spec = pltpu.PrefetchScalarGridSpec(
        num_scalar_prefetch=1,
        grid=(3, 2),
        in_specs=[
            pl.BlockSpec((1, 9, 1, 4, 8, 256), lambda a, j, x: (a, 0, (j + x[0]) % 2, 0, 0, 0))
        ],
        out_specs=pl.BlockSpec((2, 1, 2, 2, 9, 8, 128), lambda a, j, x: (0, j, 0, 0, a, 0, 0)),
    )
    return pl.pallas_call(
        pack_body,
        grid_spec=grid_spec,
        out_shape=jax.ShapeDtypeStruct((2, 2, 2, 2, 27, 8, 128), jnp.float32),
    )(x, parts)


def ring_sum(pieces, z):
    def piece(step):
        return lax.dynamic_index_in_dim(pieces, lax.rem(z + step + 8, 8), 0, False)

    up, down = piece(4), piece(-3)
    for step in (3, 2, 1):
        up = shift(up, z=1) + piece(step)
        if step > 1:
            down = shift(down, z=-1) + piece(1 - step)
    return shift(up, z=1) + shift(down, z=-1) + piece(0)


def shards(activations, out_grad):
    count, slab_x, size_y, size_z = activations.shape
    lanes = size_y * size_z
    cells = slab_x * lanes
    space, chan = lax.axis_index("space"), lax.axis_index("chan")
    z, high = space % 8, space // 8
    y, x, k = chan // 4, chan // 2 % 2, chan % 2

    grad = out_grad.reshape(count, cells)
    up = shift(grad, y=1)
    down = shift(grad, y=-1)
    acts = activations.reshape(count, cells)
    acts_near = shift(acts, x=1)
    edges = jnp.concatenate(
        [
            lax.ppermute(acts[:, cells - lanes :], "space", halo_pairs(1)),
            lax.ppermute(acts[:, :lanes], "space", halo_pairs(-1)),
        ],
        axis=1,
    )
    edges_near = shift(edges, x=1)
    half = cells // 2
    far = jnp.concatenate([shift(up[:, :half], y=1), shift(down[:, half:], y=-1)], axis=1)

    grads = jnp.zeros((8 * count, cells), grad.dtype)
    for source, block in ((0, grad), (-1, up), (1, down), (2, far)):
        row = (y + source) % 4 * 2
        grads = lax.dynamic_update_slice(grads, block, ((row + k) * count, 0))
        grads = lax.dynamic_update_slice(grads, shift(block, k=1), ((row + 1 - k) * count, 0))

    near = [
        jnp.concatenate([e[:, :lanes], v, e[:, lanes:]], axis=1)
        for e, v in ((edges, acts), (edges_near, acts_near))
    ]
    windows = windows_of(jnp.concatenate(near, axis=0), size_z, lanes)
    parts = jnp.stack(
        [
            lax.dot_general(
                windows[:, a * lanes : a * lanes + cells],
                grads,
                (((1,), (1,)), ((), ())),
                preferred_element_type=jnp.float32,
            )
            for a in range(3)
        ]
    )
    parts = parts.reshape(3, 9, 2, 4, 8, 8 * count)
    pieces = pack(parts, x.reshape(1).astype(jnp.int32)).reshape(8, 2, 27, 8, 128)
    mine = ring_sum(pieces, z)
    keep = lax.dynamic_index_in_dim(mine, high, 0, False)
    give = lax.dynamic_index_in_dim(mine, 1 - high, 0, False)

    def turned(d, flip):
        bits = d["z"]
        low = bits // 2 % 2
        return dict(d, z=bits + 2 * (d["x"] - low), x=low, h=d["h"] + flip)

    total = send(keep, lambda d: turned(d, 0)) + send(give, lambda d: turned(d, 1))
    all_cells = cells * lax.axis_size("space")
    scale = jnp.float32(1.0) / jnp.sqrt(jnp.float32(all_cells))
    total = (total * scale).reshape(27, 8, 4, count)
    return jnp.transpose(total, (0, 3, 2, 1)).reshape(27, count, count)


def solution(mesh):
    return jax.shard_map(
        shards,
        mesh=mesh,
        in_specs=(P("chan", "space", None, None), P("chan", "space", None, None)),
        out_specs=P(None, "space", "chan"),
        check_vma=False,
    )
```

```python
import functools

import jax
import jax.numpy as jnp
from jax import lax
from jax.experimental import pallas as pl
from jax.experimental.pallas import tpu as pltpu
from jax.sharding import PartitionSpec as P


AXES = ("space", "chan")
SIZES = (("h", 2), ("z", 8), ("y", 4), ("x", 2), ("k", 2))


def place(index):
    found = {}
    for name, size in reversed(SIZES):
        index, found[name] = divmod(index, size)
    return found


def index_of(found):
    index = 0
    for name, size in SIZES:
        index = index * size + found[name] % size
    return index


def send(value, move):
    pairs = [(i, index_of(move(place(i)))) for i in range(256)]
    return lax.ppermute(value, AXES, pairs)


def shift(value, **steps):
    return send(value, lambda d: {n: d[n] + steps.get(n, 0) for n in d})


def halo_pairs(step):
    count = lax.axis_size("space")
    return [(i, i + step) for i in range(count) if 0 <= i + step < count]


def spread_body(size_z, own, own_edge, near, near_edge, out_ref):
    x = pl.program_id(0)
    inside = jnp.logical_and(x > 0, x < pl.num_programs(0) - 1)
    rows, lanes = own.shape
    z = lax.broadcasted_iota(jnp.int32, (rows, lanes), 1) % size_z
    stack = []
    for middle, edge in ((own, own_edge), (near, near_edge)):
        center = jnp.where(inside, middle[...].astype(jnp.float32), edge[...].astype(jnp.float32))
        stack.append(jnp.where(z == 0, 0.0, pltpu.roll(center, 1, 1)))
        stack.append(center)
        stack.append(jnp.where(z == size_z - 1, 0.0, pltpu.roll(center, lanes - 1, 1)))
    stack += [jnp.zeros((rows, lanes), jnp.float32)] * 2
    turned = jnp.concatenate(stack, axis=0).T.astype(out_ref.dtype)
    blank = jnp.zeros((size_z, out_ref.shape[2]), out_ref.dtype)
    out_ref[0, :size_z] = blank
    out_ref[0, size_z : size_z + lanes] = turned
    out_ref[0, size_z + lanes :] = blank


def spread(own, own_edge, near, near_edge, size_z, lanes):
    rows, cells = own.shape
    slabs = cells // lanes
    middle = pl.BlockSpec((rows, lanes), lambda x: (0, jnp.clip(x - 1, 0, slabs - 1)))
    edge = pl.BlockSpec((rows, lanes), lambda x: (0, x // (slabs + 1)))
    shape = (slabs + 2, lanes + 2 * size_z, 8 * rows)
    return pl.pallas_call(
        functools.partial(spread_body, size_z),
        grid=(slabs + 2,),
        in_specs=[middle, edge, middle, edge],
        out_specs=pl.BlockSpec((1,) + shape[1:], lambda x: (x, 0, 0)),
        out_shape=jax.ShapeDtypeStruct(shape, own.dtype),
        compiler_params=pltpu.CompilerParams(vmem_limit_bytes=40 * 2**20),
        cost_estimate=pl.CostEstimate(
            flops=10 * 2**20, bytes_accessed=30 * 2**20, transcendentals=0
        ),
    )(own, own_edge, near, near_edge)


def product_body(count, slabs, size_z, *refs):
    blocks, field, out_ref = refs[:count], refs[count], refs[count + 1]
    held, total, sems = refs[count + 2 :]
    x = pl.program_id(0)
    lanes = held.shape[1] // (slabs + 4)
    rows = held.shape[0] // count

    @pl.when(x == 0)
    def _():
        copies = [
            pltpu.make_async_copy(
                block,
                held.at[pl.ds(i * rows, rows), pl.ds(2 * lanes, slabs * lanes)],
                sems.at[i],
            )
            for i, block in enumerate(blocks)
        ]
        for copy in copies:
            copy.start()
        blank = jnp.zeros((held.shape[0], 2 * lanes), held.dtype)
        held[:, : 2 * lanes] = blank
        held[:, (slabs + 2) * lanes :] = blank
        total[...] = jnp.zeros_like(total)
        for copy in copies:
            copy.wait()

    left = jnp.concatenate(
        [
            held[:, pl.ds(pl.multiple_of((x + 2 - a) * lanes, lanes), lanes)]
            for a in range(3)
        ],
        axis=0,
    )

    def step(b, carry):
        at = pl.multiple_of(b * size_z, size_z)
        total[b] += jnp.dot(
            left, field[0, pl.ds(at, lanes), :], preferred_element_type=jnp.float32
        )
        return carry

    lax.fori_loop(0, 3, step, 0)

    @pl.when(x == pl.num_programs(0) - 1)
    def _():
        for i in range(count):
            for n in range(2):
                for a in range(3):
                    for b in range(3):
                        at = (a * count + i) * rows
                        out_ref[i, n, :, (3 * a + b) * 96 : (3 * a + b + 1) * 96] = total[
                            b, at : at + rows, n * 96 : (n + 1) * 96
                        ]
                out_ref[i, n, :, 864:] = jnp.zeros((rows, 32), jnp.float32)


def product(blocks, field, size_z):
    count = len(blocks)
    rows, cells = blocks[0].shape
    slabs = field.shape[0] - 2
    lanes = cells // slabs
    return pl.pallas_call(
        functools.partial(product_body, count, slabs, size_z),
        grid=(slabs + 2,),
        in_specs=[pl.BlockSpec(memory_space=pl.ANY)] * count
        + [pl.BlockSpec((1,) + field.shape[1:], lambda x: (x, 0, 0))],
        out_specs=pl.BlockSpec((count, 2, rows, 896), lambda x: (0, 0, 0, 0)),
        out_shape=jax.ShapeDtypeStruct((count, 2, rows, 896), jnp.float32),
        scratch_shapes=[
            pltpu.VMEM((count * rows, (slabs + 4) * lanes), blocks[0].dtype),
            pltpu.VMEM((3, 3 * count * rows, field.shape[2]), jnp.float32),
            pltpu.SemaphoreType.DMA((count,)),
        ],
        compiler_params=pltpu.CompilerParams(vmem_limit_bytes=48 * 2**20),
        cost_estimate=pl.CostEstimate(
            flops=count * 2**31, bytes_accessed=20 * 2**20, transcendentals=0
        ),
    )(*blocks, field)


def ring_sum(piece):
    up, down = piece(4), piece(-3)
    for step in (3, 2, 1):
        up = shift(up, z=1) + piece(step)
        if step > 1:
            down = shift(down, z=-1) + piece(1 - step)
    return shift(up, z=1) + shift(down, z=-1) + piece(0)


def shards(activations, out_grad):
    count, slab_x, size_y, size_z = activations.shape
    lanes = size_y * size_z
    cells = slab_x * lanes
    half = cells // 2
    space, chan = lax.axis_index("space"), lax.axis_index("chan")
    z, high = space % 8, space // 8
    y, x, k = chan // 4, chan // 2 % 2, chan % 2

    grad = out_grad.reshape(count, cells)
    grad, activations = lax.optimization_barrier((grad, activations))
    up, down = shift(grad, y=1), shift(grad, y=-1)
    acts = activations.reshape(count, cells)
    acts_near = shift(acts, x=1)
    edges = jnp.concatenate(
        [
            lax.ppermute(acts[:, cells - lanes :], "space", halo_pairs(1)),
            lax.ppermute(acts[:, :lanes], "space", halo_pairs(-1)),
        ],
        axis=1,
    )
    edges_near = shift(edges, x=1)
    far_up, far_down = shift(up[:, :half], y=1), shift(down[:, half:], y=-1)
    far = jnp.concatenate([far_up, far_down], axis=1)

    field = spread(acts, edges, acts_near, edges_near, size_z, lanes)
    blocks = []
    for block in (grad, down, far, up):
        blocks += [block, shift(block, k=1)]
    parts = product(blocks, field, size_z)

    def piece(step):
        to = lax.rem(z + step + 8, 8)
        b, j, c = to // 4, to // 2 % 2, to % 2
        return jnp.stack(
            [
                lax.dynamic_slice(
                    parts,
                    ((2 * h + b - y) % 4 * 2 + (c ^ k), j ^ x, 0, 0),
                    (1, 1) + parts.shape[2:],
                )[0, 0]
                for h in range(2)
            ]
        )

    mine = ring_sum(piece)
    keep = lax.dynamic_index_in_dim(mine, high, 0, False)
    give = lax.dynamic_index_in_dim(mine, 1 - high, 0, False)

    def turned(d, flip):
        bits = d["z"]
        low = bits // 2 % 2
        return dict(d, z=bits + 2 * (d["x"] - low), x=low, h=d["h"] + flip)

    total = send(keep, lambda d: turned(d, 0)) + send(give, lambda d: turned(d, 1))
    scale = jnp.float32(1.0) / jnp.sqrt(jnp.float32(cells * lax.axis_size("space")))
    total = (total[:, : 27 * count] * scale).reshape(count, 27, count)
    return jnp.transpose(total, (1, 0, 2))


def solution(mesh):
    return jax.shard_map(
        shards,
        mesh=mesh,
        in_specs=(P("chan", "space", None, None), P("chan", "space", None, None)),
        out_specs=P(None, "space", "chan"),
        check_vma=False,
    )
```

```python
import functools

import jax
import jax.numpy as jnp
from jax import lax
from jax.experimental import pallas as pl
from jax.experimental.pallas import tpu as pltpu
from jax.sharding import PartitionSpec as P


AXES = ("space", "chan")
SIZES = (("h", 2), ("z", 8), ("y", 4), ("x", 2), ("k", 2))


def place(index):
    found = {}
    for name, size in reversed(SIZES):
        index, found[name] = divmod(index, size)
    return found


def index_of(found):
    index = 0
    for name, size in SIZES:
        index = index * size + found[name] % size
    return index


def send(value, move):
    pairs = [(i, index_of(move(place(i)))) for i in range(256)]
    return lax.ppermute(value, AXES, pairs)


def shift(value, **steps):
    return send(value, lambda d: {n: d[n] + steps.get(n, 0) for n in d})


def halo_pairs(step):
    count = lax.axis_size("space")
    return [(i, i + step) for i in range(count) if 0 <= i + step < count]


def spread_body(size_z, own, own_edge, near, near_edge, out_ref):
    x = pl.program_id(0)
    inside = jnp.logical_and(x > 0, x < pl.num_programs(0) - 1)
    rows, lanes = own.shape
    z = lax.broadcasted_iota(jnp.int32, (rows, lanes), 1) % size_z
    stack = []
    for middle, edge in ((own, own_edge), (near, near_edge)):
        center = jnp.where(inside, middle[...].astype(jnp.float32), edge[...].astype(jnp.float32))
        stack.append(jnp.where(z == 0, 0.0, pltpu.roll(center, 1, 1)))
        stack.append(center)
        stack.append(jnp.where(z == size_z - 1, 0.0, pltpu.roll(center, lanes - 1, 1)))
    stack += [jnp.zeros((rows, lanes), jnp.float32)] * 2
    turned = jnp.concatenate(stack, axis=0).T.astype(out_ref.dtype)
    blank = jnp.zeros((size_z, out_ref.shape[2]), out_ref.dtype)
    out_ref[0, :size_z] = blank
    out_ref[0, size_z : size_z + lanes] = turned
    out_ref[0, size_z + lanes :] = blank


def spread(own, own_edge, near, near_edge, size_z, lanes):
    rows, cells = own.shape
    slabs = cells // lanes
    middle = pl.BlockSpec((rows, lanes), lambda x: (0, jnp.clip(x - 1, 0, slabs - 1)))
    edge = pl.BlockSpec((rows, lanes), lambda x: (0, x // (slabs + 1)))
    shape = (slabs + 2, lanes + 2 * size_z, 8 * rows)
    return pl.pallas_call(
        functools.partial(spread_body, size_z),
        grid=(slabs + 2,),
        in_specs=[middle, edge, middle, edge],
        out_specs=pl.BlockSpec((1,) + shape[1:], lambda x: (x, 0, 0)),
        out_shape=jax.ShapeDtypeStruct(shape, own.dtype),
        compiler_params=pltpu.CompilerParams(vmem_limit_bytes=20 * 2**20),
        cost_estimate=pl.CostEstimate(
            flops=10 * 2**20, bytes_accessed=30 * 2**20, transcendentals=0
        ),
    )(own, own_edge, near, near_edge)


def product_body(count, slabs, size_z, lines, *refs):
    blocks, field, out_ref = refs[:count], refs[count], refs[count + 1]
    held, total, sems = refs[count + 2 :]
    x = pl.program_id(0)
    lanes = held.shape[1] // slabs
    rows = held.shape[0] // count
    tall = count * rows

    @pl.when(x == 0)
    def _():
        copies = [
            pltpu.make_async_copy(block, held.at[pl.ds(i * rows, rows), :], sems.at[i])
            for i, block in enumerate(blocks)
        ]
        for copy in copies:
            copy.start()
        total[...] = jnp.zeros_like(total)
        for copy in copies:
            copy.wait()

    def add(first, last):
        left = jnp.concatenate(
            [
                held[:, pl.ds(pl.multiple_of((x - a) * lanes, lanes), lanes)]
                for a in range(first, last)
            ],
            axis=0,
        )
        for i, b in enumerate(lines):
            total[i, first * tall : last * tall] += jnp.dot(
                left,
                field[0, b * size_z : b * size_z + lanes, :],
                preferred_element_type=jnp.float32,
            )

    for first, last, chosen in (
        (0, 1, x == 0),
        (0, 2, x == 1),
        (0, 3, jnp.logical_and(x > 1, x < slabs)),
        (1, 3, x == slabs),
        (2, 3, x == slabs + 1),
    ):
        pl.when(chosen)(functools.partial(add, first, last))

    @pl.when(x == slabs + 1)
    def _():
        for block in range(count):
            for n in range(2):
                for i in range(len(lines)):
                    for a in range(3):
                        at = a * tall + block * rows
                        to = (3 * i + a) * 96
                        out_ref[block, n, :, to : to + 96] = total[
                            i, at : at + rows, n * 96 : (n + 1) * 96
                        ]
                end = len(lines) * 288
                out_ref[block, n, :, end:] = jnp.zeros(
                    (rows, out_ref.shape[3] - end), jnp.float32
                )


def product(blocks, field, size_z, lines):
    count = len(blocks)
    rows, cells = blocks[0].shape
    slabs = field.shape[0] - 2
    lanes = cells // slabs
    wide = -(-len(lines) * 288 // 128) * 128
    return pl.pallas_call(
        functools.partial(product_body, count, slabs, size_z, lines),
        grid=(slabs + 2,),
        in_specs=[pl.BlockSpec(memory_space=pl.ANY)] * count
        + [pl.BlockSpec((1,) + field.shape[1:], lambda x: (x, 0, 0))],
        out_specs=pl.BlockSpec((count, 2, rows, wide), lambda x: (0, 0, 0, 0)),
        out_shape=jax.ShapeDtypeStruct((count, 2, rows, wide), jnp.float32),
        scratch_shapes=[
            pltpu.VMEM((count * rows, cells), blocks[0].dtype),
            pltpu.VMEM((len(lines), 3 * count * rows, field.shape[2]), jnp.float32),
            pltpu.SemaphoreType.DMA((count,)),
        ],
        compiler_params=pltpu.CompilerParams(vmem_limit_bytes=14 * 2**20),
        cost_estimate=pl.CostEstimate(
            flops=count * len(lines) * 10**9, bytes_accessed=16 * 2**20, transcendentals=0
        ),
    )(*blocks, field)


def ring_step(piece, step, up, down):
    if step < 3:
        up = up + piece(step + 1)
        down = down + piece(-step)
    return shift(up, z=1), shift(down, z=-1)


def shards(activations, out_grad):
    count, slab_x, size_y, size_z = activations.shape
    lanes = size_y * size_z
    cells = slab_x * lanes
    half = cells // 2
    space, chan = lax.axis_index("space"), lax.axis_index("chan")
    z, high = space % 8, space // 8
    y, x, k = chan // 4, chan // 2 % 2, chan % 2

    def cross(value, bits):
        return send(value, lambda d: dict(d, y=d["y"] ^ bits))

    grad = out_grad.reshape(count, cells)
    grad, activations = lax.optimization_barrier((grad, activations))
    next_y, last_y = cross(grad, 1), cross(grad, 3)
    acts = activations.reshape(count, cells)
    acts_near = shift(acts, x=1)
    before = lax.ppermute(acts[:, cells - lanes :], "space", halo_pairs(1))
    after = lax.ppermute(acts[:, :lanes], "space", halo_pairs(-1))
    grad_mate = shift(grad, k=1)
    next_y, last_y, acts_near, before, after, grad_mate = lax.optimization_barrier(
        (next_y, last_y, acts_near, before, after, grad_mate)
    )
    far_one, far_two = cross(next_y[:, :half], 3), cross(last_y[:, half:], 1)
    edges = jnp.concatenate([before, after], axis=1)
    edges_near = shift(edges, x=1)
    next_mate, last_mate = shift(next_y, k=1), shift(last_y, k=1)

    field = spread(acts, edges, acts_near, edges_near, size_z, lanes)
    parts_near = product((grad, grad_mate, next_y, next_mate), field, size_z, (0, 1, 2))
    far_one, far_two, parts_near = lax.optimization_barrier((far_one, far_two, parts_near))
    far = jnp.concatenate([far_one, far_two], axis=1)
    others = (far, shift(far, k=1), last_y, last_mate)

    def taken(parts, step):
        to = lax.rem(z + step + 8, 8)
        b, j, c = to // 4, to // 2 % 2, to % 2
        at = ((b ^ (y % 2)) * 2 + (c ^ k), j ^ x, 0, 0)
        return lax.dynamic_slice(parts, at, (1, 1) + parts.shape[2:])[0, 0]

    piece_near = functools.partial(taken, parts_near)
    up, down = piece_near(4), piece_near(-3)
    parts_far = []
    for b in range(3):
        up, down = ring_step(piece_near, 3 - b, up, down)
        part = product(others, field, size_z, (b,))
        up, down, part, field = lax.optimization_barrier((up, down, part, field))
        parts_far.append(part)
    mine_near = piece_near(0) + down
    up_near = shift(up + piece_near(1), z=1)

    def piece_far(step):
        columns = [taken(parts, step)[:, :288] for parts in parts_far]
        return jnp.concatenate(columns + [jnp.zeros((count, 32), jnp.float32)], axis=1)

    up, down = piece_far(4), piece_far(-3)
    for step in (3, 2, 1):
        up, down = ring_step(piece_far, step, up, down)
        up, down, up_near = lax.optimization_barrier((up, down, up_near))
    mine_near = mine_near + up_near
    mine_far = piece_far(0) + down + shift(up + piece_far(1), z=1)
    here = high == y // 2
    keep = jnp.where(here, mine_near, mine_far)
    give = jnp.where(here, mine_far, mine_near)

    def turned(d, flip):
        bits = d["z"]
        low = bits // 2 % 2
        return dict(d, z=bits + 2 * (d["x"] - low), x=low, h=d["h"] + flip)

    total = send(keep, lambda d: turned(d, 0)) + send(give, lambda d: turned(d, 1))
    scale = jnp.float32(1.0) / jnp.sqrt(jnp.float32(cells * lax.axis_size("space")))
    total = (total[:, : 27 * count] * scale).reshape(count, 3, 3, 3, count)
    return jnp.transpose(total, (2, 1, 3, 0, 4)).reshape(27, count, count)


def solution(mesh):
    return jax.shard_map(
        shards,
        mesh=mesh,
        in_specs=(P("chan", "space", None, None), P("chan", "space", None, None)),
        out_specs=P(None, "space", "chan"),
        check_vma=False,
    )
```

```python
import functools

import jax
import jax.numpy as jnp
from jax import lax
from jax.experimental import pallas as pl
from jax.experimental.pallas import tpu as pltpu
from jax.sharding import PartitionSpec as P


AXES = ("space", "chan")
VMEM = 52 * 2**20
SIZES = (("h", 2), ("z", 8), ("y", 4), ("x", 2), ("k", 2))


def place(index):
    found = {}
    for name, size in reversed(SIZES):
        index, found[name] = divmod(index, size)
    return found


def index_of(found):
    index = 0
    for name, size in SIZES:
        index = index * size + found[name] % size
    return index


def send(value, move):
    pairs = [(i, index_of(move(place(i)))) for i in range(256)]
    return lax.ppermute(value, AXES, pairs)


def shift(value, **steps):
    return send(value, lambda d: {n: d[n] + steps.get(n, 0) for n in d})


def halo_pairs(step):
    count = lax.axis_size("space")
    return [(i, i + step) for i in range(count) if 0 <= i + step < count]


def spread_body(size_z, middle, edge, out_ref):
    x = pl.program_id(0)
    inside = jnp.logical_and(x > 0, x < pl.num_programs(0) - 1)
    rows, lanes = middle.shape
    z = lax.broadcasted_iota(jnp.int32, (rows, lanes), 1) % size_z
    center = jnp.where(inside, middle[...].astype(jnp.float32), edge[...].astype(jnp.float32))
    below = jnp.where(z == 0, 0.0, pltpu.roll(center, 1, 1))
    above = jnp.where(z == size_z - 1, 0.0, pltpu.roll(center, lanes - 1, 1))
    stack = [below, center, above, jnp.zeros((rows, lanes), jnp.float32)]
    turned = jnp.concatenate(stack, axis=0).T.astype(out_ref.dtype)
    blank = jnp.zeros((size_z, out_ref.shape[2]), out_ref.dtype)
    out_ref[0, :size_z] = blank
    out_ref[0, size_z : size_z + lanes] = turned
    out_ref[0, size_z + lanes :] = blank


def spread(cells, edges, size_z, lanes):
    rows, total = cells.shape
    slabs = total // lanes
    shape = (slabs + 2, lanes + 2 * size_z, 4 * rows)
    return pl.pallas_call(
        functools.partial(spread_body, size_z),
        grid=(slabs + 2,),
        in_specs=[
            pl.BlockSpec((rows, lanes), lambda x: (0, jnp.clip(x - 1, 0, slabs - 1))),
            pl.BlockSpec((rows, lanes), lambda x: (0, x // (slabs + 1))),
        ],
        out_specs=pl.BlockSpec((1,) + shape[1:], lambda x: (x, 0, 0)),
        out_shape=jax.ShapeDtypeStruct(shape, cells.dtype),
        compiler_params=pltpu.CompilerParams(vmem_limit_bytes=VMEM),
        cost_estimate=pl.CostEstimate(
            flops=10 * 2**20, bytes_accessed=10 * 2**20, transcendentals=0
        ),
    )(cells, edges)


def product_body(cuts, slabs, size_z, *refs):
    count = len(cuts)
    refs = list(refs)
    blocks = [[refs.pop(0) for _ in range(cut)] for cut in cuts]
    own, near, out_ref, held, total, sems = refs
    x = pl.program_id(0)
    lanes = held.shape[1] // slabs
    rows = held.shape[0] // count
    tall = count * rows

    @pl.when(x == 0)
    def _():
        copies = []
        for i, parts in enumerate(blocks):
            width = held.shape[1] // len(parts)
            for j, part in enumerate(parts):
                to = held.at[pl.ds(i * rows, rows), pl.ds(j * width, width)]
                copies.append(pltpu.make_async_copy(part, to, sems.at[len(copies)]))
        for copy in copies:
            copy.start()
        total[...] = jnp.zeros_like(total)
        for copy in copies:
            copy.wait()

    def add(first, last):
        left = jnp.concatenate(
            [
                held[:, pl.ds(pl.multiple_of((x - a) * lanes, lanes), lanes)]
                for a in range(first, last)
            ],
            axis=0,
        )
        for b in range(3):
            at = slice(b * size_z, b * size_z + lanes)
            total[b, first * tall : last * tall] += jnp.dot(
                left,
                jnp.concatenate([own[0, at, :], near[0, at, :]], axis=1),
                preferred_element_type=jnp.float32,
            )

    for first, last, chosen in (
        (0, 1, x == 0),
        (0, 2, x == 1),
        (0, 3, jnp.logical_and(x > 1, x < slabs)),
        (1, 3, x == slabs),
        (2, 3, x == slabs + 1),
    ):
        pl.when(chosen)(functools.partial(add, first, last))

    @pl.when(x == slabs + 1)
    def _():
        for block in range(count):
            for n in range(2):
                for a in range(3):
                    for b in range(3):
                        at = a * tall + block * rows
                        to = (3 * a + b) * 96
                        out_ref[block, n, :, to : to + 96] = total[
                            b, at : at + rows, n * 128 : n * 128 + 96
                        ]
                out_ref[block, n, :, 864:] = jnp.zeros((rows, 32), jnp.float32)


def product(blocks, own, near, size_z):
    count = len(blocks)
    rows = blocks[0][0].shape[0]
    slabs = own.shape[0] - 2
    cells = slabs * (own.shape[1] - 2 * size_z)
    cuts = tuple(len(parts) for parts in blocks)
    field = pl.BlockSpec((1,) + own.shape[1:], lambda x: (x, 0, 0))
    return pl.pallas_call(
        functools.partial(product_body, cuts, slabs, size_z),
        grid=(slabs + 2,),
        in_specs=[pl.BlockSpec(memory_space=pl.ANY)] * sum(cuts) + [field, field],
        out_specs=pl.BlockSpec((count, 2, rows, 896), lambda x: (0, 0, 0, 0)),
        out_shape=jax.ShapeDtypeStruct((count, 2, rows, 896), jnp.float32),
        scratch_shapes=[
            pltpu.VMEM((count * rows, cells), own.dtype),
            pltpu.VMEM((3, 3 * count * rows, 2 * own.shape[2]), jnp.float32),
            pltpu.SemaphoreType.DMA((sum(cuts),)),
        ],
        compiler_params=pltpu.CompilerParams(vmem_limit_bytes=VMEM),
        cost_estimate=pl.CostEstimate(
            flops=count * 3 * 10**9, bytes_accessed=16 * 2**20, transcendentals=0
        ),
    )(*[part for parts in blocks for part in parts], own, near)


def ring_sum(piece):
    up, down = piece(4), piece(-3)
    for step in (3, 2, 1):
        up = shift(up, z=1) + piece(step)
        if step > 1:
            down = shift(down, z=-1) + piece(1 - step)
        up, down = lax.optimization_barrier((up, down))
    return shift(up, z=1) + shift(down, z=-1) + piece(0)


def shards(activations, out_grad):
    count, slab_x, size_y, size_z = activations.shape
    lanes = size_y * size_z
    cells = slab_x * lanes
    half = cells // 2
    space, chan = lax.axis_index("space"), lax.axis_index("chan")
    z, high = space % 8, space // 8
    y, x, k = chan // 4, chan // 2 % 2, chan % 2

    def cross(value, bits):
        return send(value, lambda d: dict(d, y=d["y"] ^ bits))

    grad = out_grad.reshape(count, cells)
    grad, activations = lax.optimization_barrier((grad, activations))
    next_y, last_y = cross(grad, 1), cross(grad, 3)
    acts = activations.reshape(count, cells)
    acts_near = shift(acts, x=1)
    before = lax.ppermute(acts[:, cells - lanes :], "space", halo_pairs(1))
    after = lax.ppermute(acts[:, :lanes], "space", halo_pairs(-1))
    grad_mate = shift(grad, k=1)
    edges = jnp.concatenate([before, after], axis=1)
    own = spread(acts, edges, size_z, lanes)
    next_y, last_y, edges, own = lax.optimization_barrier((next_y, last_y, edges, own))
    far_one, far_two = cross(next_y[:, :half], 3), cross(last_y[:, half:], 1)
    edges_near = shift(edges, x=1)
    next_mate, last_mate = shift(next_y, k=1), shift(last_y, k=1)

    near = spread(acts_near, edges_near, size_z, lanes)
    far_one, far_two, near, grad_mate, next_mate, last_mate = lax.optimization_barrier(
        (far_one, far_two, near, grad_mate, next_mate, last_mate)
    )
    far_mate = shift(far_one, k=1), shift(far_two, k=1)
    first = product(((grad,), (grad_mate,), (next_y,), (next_mate,)), own, near, size_z)
    first, near = lax.optimization_barrier((first, near))
    second = product(((far_one, far_two), far_mate, (last_y,), (last_mate,)), own, near, size_z)

    def piece(step):
        to = lax.rem(z + step + 8, 8)
        b, j, c = to // 4, to // 2 % 2, to % 2
        at = ((b ^ (y % 2)) * 2 + (c ^ k), j ^ x, 0, 0)
        size = (1, 1) + first.shape[2:]
        return jnp.stack([lax.dynamic_slice(part, at, size)[0, 0] for part in (first, second)])

    mine = ring_sum(piece)
    here = (high == y // 2).astype(jnp.int32)
    keep = lax.dynamic_index_in_dim(mine, 1 - here, 0, False)
    give = lax.dynamic_index_in_dim(mine, here, 0, False)

    def turned(d, flip):
        bits = d["z"]
        low = bits // 2 % 2
        return dict(d, z=bits + 2 * (d["x"] - low), x=low, h=d["h"] + flip)

    total = send(keep, lambda d: turned(d, 0)) + send(give, lambda d: turned(d, 1))
    scale = jnp.float32(1.0) / jnp.sqrt(jnp.float32(cells * lax.axis_size("space")))
    total = (total[:, : 27 * count] * scale).reshape(count, 27, count)
    return jnp.transpose(total, (1, 0, 2))


def solution(mesh):
    return jax.shard_map(
        shards,
        mesh=mesh,
        in_specs=(P("chan", "space", None, None), P("chan", "space", None, None)),
        out_specs=P(None, "space", "chan"),
        check_vma=False,
    )
```

```python
import functools

import jax
import jax.numpy as jnp
from jax import lax
from jax.experimental import pallas as pl
from jax.experimental.pallas import tpu as pltpu
from jax.sharding import PartitionSpec as P


AXES = ("space", "chan")
VMEM = 52 * 2**20
SIZES = (("h", 2), ("z", 8), ("y", 4), ("x", 2), ("k", 2))


def place(index):
    found = {}
    for name, size in reversed(SIZES):
        index, found[name] = divmod(index, size)
    return found


def index_of(found):
    index = 0
    for name, size in SIZES:
        index = index * size + found[name] % size
    return index


def send(value, move):
    pairs = [(i, index_of(move(place(i)))) for i in range(256)]
    return lax.ppermute(value, AXES, pairs)


def shift(value, **steps):
    return send(value, lambda d: {n: d[n] + steps.get(n, 0) for n in d})


def spread_body(size_z, slabs, lanes, middle, edge, out_ref):
    rows = middle.shape[0]
    z = lax.broadcasted_iota(jnp.int32, (rows, lanes), 1) % size_z
    blank = jnp.zeros((size_z, out_ref.shape[2]), out_ref.dtype)
    for part in range(out_ref.shape[0]):
        x = pl.program_id(0) * out_ref.shape[0] + part
        inside = jnp.logical_and(x > 0, x <= slabs)
        at = pl.multiple_of(jnp.clip(x - 1, 0, slabs - 1) * lanes, lanes)
        side = pl.multiple_of(x // (slabs + 1) * lanes, lanes)
        center = jnp.where(
            inside,
            middle[:, pl.ds(at, lanes)].astype(jnp.float32),
            edge[:, pl.ds(side, lanes)].astype(jnp.float32),
        )
        below = jnp.where(z == 0, 0.0, pltpu.roll(center, 1, 1))
        above = jnp.where(z == size_z - 1, 0.0, pltpu.roll(center, lanes - 1, 1))
        stack = [below, center, above, jnp.zeros((rows, lanes), jnp.float32)]
        turned = jnp.concatenate(stack, axis=0).T.astype(out_ref.dtype)
        out_ref[part, :size_z] = blank
        out_ref[part, size_z : size_z + lanes] = turned
        out_ref[part, size_z + lanes :] = blank


def spread(cells, edges, size_z, lanes):
    rows, total = cells.shape
    slabs = total // lanes
    shape = (slabs + 2, lanes + 2 * size_z, 4 * rows)
    return pl.pallas_call(
        functools.partial(spread_body, size_z, slabs, lanes),
        grid=((slabs + 2) // 2,),
        in_specs=[
            pl.BlockSpec(cells.shape, lambda x: (0, 0)),
            pl.BlockSpec(edges.shape, lambda x: (0, 0)),
        ],
        out_specs=pl.BlockSpec((2,) + shape[1:], lambda x: (x, 0, 0)),
        out_shape=jax.ShapeDtypeStruct(shape, cells.dtype),
        compiler_params=pltpu.CompilerParams(vmem_limit_bytes=VMEM),
        cost_estimate=pl.CostEstimate(
            flops=10 * 2**20, bytes_accessed=10 * 2**20, transcendentals=0
        ),
    )(cells, edges)


def product_body(cuts, slabs, size_z, *refs):
    count = len(cuts)
    refs = list(refs)
    blocks = [[refs.pop(0) for _ in range(cut)] for cut in cuts]
    own, near, out_ref, held, total, sems = refs
    x = pl.program_id(0)
    lanes = held.shape[1] // slabs
    rows = held.shape[0] // count
    tall = count * rows

    @pl.when(x == 0)
    def _():
        copies = []
        for i, parts in enumerate(blocks):
            width = held.shape[1] // len(parts)
            for j, part in enumerate(parts):
                to = held.at[pl.ds(i * rows, rows), pl.ds(j * width, width)]
                copies.append(pltpu.make_async_copy(part, to, sems.at[len(copies)]))
        for copy in copies:
            copy.start()
        total[...] = jnp.zeros_like(total)
        for copy in copies:
            copy.wait()

    def add(first, last):
        left = jnp.concatenate(
            [
                held[:, pl.ds(pl.multiple_of((x - a) * lanes, lanes), lanes)]
                for a in range(first, last)
            ],
            axis=0,
        )
        for b in range(3):
            at = slice(b * size_z, b * size_z + lanes)
            total[b, first * tall : last * tall] += jnp.dot(
                left,
                jnp.concatenate([own[0, at, :], near[0, at, :]], axis=1),
                preferred_element_type=jnp.float32,
            )

    for first, last, chosen in (
        (0, 1, x == 0),
        (0, 2, x == 1),
        (0, 3, jnp.logical_and(x > 1, x < slabs)),
        (1, 3, x == slabs),
        (2, 3, x == slabs + 1),
    ):
        pl.when(chosen)(functools.partial(add, first, last))

    @pl.when(x == slabs + 1)
    def _():
        for block in range(count):
            for n in range(2):
                for a in range(3):
                    for b in range(3):
                        at = a * tall + block * rows
                        to = (3 * a + b) * 96
                        out_ref[block, n, :, to : to + 96] = total[
                            b, at : at + rows, n * 128 : n * 128 + 96
                        ]
                out_ref[block, n, :, 864:] = jnp.zeros((rows, 32), jnp.float32)


def product(blocks, own, near, size_z):
    count = len(blocks)
    rows = blocks[0][0].shape[0]
    slabs = own.shape[0] - 2
    cells = slabs * (own.shape[1] - 2 * size_z)
    cuts = tuple(len(parts) for parts in blocks)
    field = pl.BlockSpec((1,) + own.shape[1:], lambda x: (x, 0, 0))
    return pl.pallas_call(
        functools.partial(product_body, cuts, slabs, size_z),
        grid=(slabs + 2,),
        in_specs=[pl.BlockSpec(memory_space=pl.ANY)] * sum(cuts) + [field, field],
        out_specs=pl.BlockSpec((count, 2, rows, 896), lambda x: (0, 0, 0, 0)),
        out_shape=jax.ShapeDtypeStruct((count, 2, rows, 896), jnp.float32),
        scratch_shapes=[
            pltpu.VMEM((count * rows, cells), own.dtype),
            pltpu.VMEM((3, 3 * count * rows, 2 * own.shape[2]), jnp.float32),
            pltpu.SemaphoreType.DMA((sum(cuts),)),
        ],
        compiler_params=pltpu.CompilerParams(vmem_limit_bytes=VMEM),
        cost_estimate=pl.CostEstimate(
            flops=count * 3 * 10**9, bytes_accessed=16 * 2**20, transcendentals=0
        ),
    )(*[part for parts in blocks for part in parts], own, near)


def ring_sum(piece):
    up, down = piece(4), piece(-3)
    for step in (3, 2, 1):
        up = shift(up, z=1) + piece(step)
        if step > 1:
            down = shift(down, z=-1) + piece(1 - step)
        up, down = lax.optimization_barrier((up, down))
    return shift(up, z=1) + shift(down, z=-1) + piece(0)


def shards(activations, out_grad):
    count, slab_x, size_y, size_z = activations.shape
    lanes = size_y * size_z
    cells = slab_x * lanes
    half = cells // 2
    space, chan = lax.axis_index("space"), lax.axis_index("chan")
    z, high = space % 8, space // 8
    y, x, k = chan // 4, chan // 2 % 2, chan % 2

    def cross(value, bits):
        return send(value, lambda d: dict(d, y=d["y"] ^ bits))

    cut = slab_x // 2
    one = out_grad[:, :cut].reshape(count, half)
    one, out_grad = lax.optimization_barrier((one, out_grad))
    next_one = cross(one, 1)
    two = out_grad[:, cut:].reshape(count, half)
    two, activations = lax.optimization_barrier((two, activations))
    last_two = cross(two, 3)
    next_two, last_one = cross(two, 1), cross(one, 3)
    acts = activations.reshape(count, cells)
    acts_near = send(acts, lambda d: dict(d, x=d["x"] ^ 1))

    def ends(flip):
        def move(value, step):
            pairs = []
            for i in range(256):
                d = place(i)
                space_to = d["h"] * 8 + d["z"] + step
                if 0 <= space_to < 16:
                    to = dict(d, h=space_to // 8, z=space_to % 8, x=d["x"] ^ flip)
                    pairs.append((i, index_of(to)))
            return lax.ppermute(value, AXES, pairs)

        return move(acts[:, cells - lanes :], 1), move(acts[:, :lanes], -1)

    own_ends, near_ends = ends(0), ends(1)
    next_one, last_two, own_ends = lax.optimization_barrier((next_one, last_two, own_ends))
    far_one, far_two = cross(next_one, 3), cross(last_two, 1)
    own = spread(acts, jnp.concatenate(own_ends, axis=1), size_z, lanes)
    next_one, last_two, next_two, last_one, own = lax.optimization_barrier(
        (next_one, last_two, next_two, last_one, own)
    )
    mates = [shift(v, k=1) for v in (one, two, next_one, last_two, next_two, last_one)]
    far_one, far_two, acts_near, near_ends, own, mates = lax.optimization_barrier(
        (far_one, far_two, acts_near, near_ends, own, mates)
    )
    far_mate = shift(far_one, k=1), shift(far_two, k=1)
    near = spread(acts_near, jnp.concatenate(near_ends, axis=1), size_z, lanes)
    blocks = (
        (one, two),
        (mates[0], mates[1]),
        (next_one, next_two),
        (mates[2], mates[4]),
        (far_one, far_two),
        far_mate,
        (last_one, last_two),
        (mates[5], mates[3]),
    )
    parts = product(blocks, own, near, size_z)

    def piece(step):
        to = lax.rem(z + step + 8, 8)
        b, j, c = to // 4, to // 2 % 2, to % 2
        at = (0, (b ^ (y % 2)) * 2 + (c ^ k), j ^ x, 0, 0)
        split = parts.reshape((2, 4) + parts.shape[1:])
        return lax.dynamic_slice(split, at, (2, 1, 1) + parts.shape[2:])[:, 0, 0]

    mine = ring_sum(piece)
    here = (high == y // 2).astype(jnp.int32)
    keep = lax.dynamic_index_in_dim(mine, 1 - here, 0, False)
    give = lax.dynamic_index_in_dim(mine, here, 0, False)

    def turned(d, flip):
        bits = d["z"]
        low = bits // 2 % 2
        return dict(d, z=bits + 2 * (d["x"] - low), x=low, h=d["h"] + flip)

    total = send(keep, lambda d: turned(d, 0)) + send(give, lambda d: turned(d, 1))
    scale = jnp.float32(1.0) / jnp.sqrt(jnp.float32(cells * lax.axis_size("space")))
    total = (total[:, : 27 * count] * scale).reshape(count, 27, count)
    return jnp.transpose(total, (1, 0, 2))


def solution(mesh):
    return jax.shard_map(
        shards,
        mesh=mesh,
        in_specs=(P("chan", "space", None, None), P("chan", "space", None, None)),
        out_specs=P(None, "space", "chan"),
        check_vma=False,
    )
```

```python
import functools

import jax
import jax.numpy as jnp
from jax import lax
from jax.experimental import pallas as pl
from jax.experimental.pallas import tpu as pltpu
from jax.sharding import PartitionSpec as P


AXES = ("space", "chan")
VMEM = 52 * 2**20
SIZES = (("h", 2), ("z", 8), ("y", 4), ("x", 2), ("k", 2))


def place(index):
    found = {}
    for name, size in reversed(SIZES):
        index, found[name] = divmod(index, size)
    return found


def index_of(found):
    index = 0
    for name, size in SIZES:
        index = index * size + found[name] % size
    return index


def send(value, move):
    pairs = [(i, index_of(move(place(i)))) for i in range(256)]
    return lax.ppermute(value, AXES, pairs)


def shift(value, **steps):
    return send(value, lambda d: {n: d[n] + steps.get(n, 0) for n in d})


def spread_body(size_z, slabs, lanes, middle, edge, out_ref):
    rows = middle.shape[0]
    z = lax.broadcasted_iota(jnp.int32, (rows, lanes), 1) % size_z
    blank = jnp.zeros((size_z, out_ref.shape[2]), out_ref.dtype)
    for part in range(out_ref.shape[0]):
        x = pl.program_id(0) * out_ref.shape[0] + part
        inside = jnp.logical_and(x > 0, x <= slabs)
        at = pl.multiple_of(jnp.clip(x - 1, 0, slabs - 1) * lanes, lanes)
        side = pl.multiple_of(x // (slabs + 1) * lanes, lanes)
        center = jnp.where(
            inside,
            middle[:, pl.ds(at, lanes)].astype(jnp.float32),
            edge[:, pl.ds(side, lanes)].astype(jnp.float32),
        )
        below = jnp.where(z == 0, 0.0, pltpu.roll(center, 1, 1))
        above = jnp.where(z == size_z - 1, 0.0, pltpu.roll(center, lanes - 1, 1))
        stack = [below, center, above, jnp.zeros((rows, lanes), jnp.float32)]
        turned = jnp.concatenate(stack, axis=0).T.astype(out_ref.dtype)
        out_ref[part, :size_z] = blank
        out_ref[part, size_z : size_z + lanes] = turned
        out_ref[part, size_z + lanes :] = blank


def spread(cells, edges, size_z, lanes):
    rows, total = cells.shape
    slabs = total // lanes
    shape = (slabs + 2, lanes + 2 * size_z, 4 * rows)
    return pl.pallas_call(
        functools.partial(spread_body, size_z, slabs, lanes),
        grid=((slabs + 2) // 2,),
        in_specs=[
            pl.BlockSpec(cells.shape, lambda x: (0, 0)),
            pl.BlockSpec(edges.shape, lambda x: (0, 0)),
        ],
        out_specs=pl.BlockSpec((2,) + shape[1:], lambda x: (x, 0, 0)),
        out_shape=jax.ShapeDtypeStruct(shape, cells.dtype),
        compiler_params=pltpu.CompilerParams(vmem_limit_bytes=VMEM),
        cost_estimate=pl.CostEstimate(
            flops=10 * 2**20, bytes_accessed=10 * 2**20, transcendentals=0
        ),
    )(cells, edges)


def product_body(cuts, slabs, size_z, terms, field_count, *refs):
    count = len(cuts)
    refs = list(refs)
    blocks = [[refs.pop(0) for _ in range(cut)] for cut in cuts]
    fields = [refs.pop(0) for _ in range(field_count)]
    sems = refs.pop()
    held = refs.pop()
    if field_count > 1:
        early, out_ref, *totals = refs
    else:
        totals = refs
    x = pl.program_id(0)
    lanes = held.shape[1] // slabs
    rows = held.shape[0] // count

    def arrivals(at):
        copies = []
        for i, parts in enumerate(blocks):
            part, inner = divmod(at, slabs // len(parts))
            copies.append(
                pltpu.make_async_copy(
                    parts[part].at[:, pl.ds(inner * lanes, lanes)],
                    held.at[pl.ds(i * rows, rows), pl.ds(at * lanes, lanes)],
                    sems.at[i, at],
                )
            )
        return copies

    @pl.when(x == 0)
    def _():
        for at in range(slabs):
            for copy in arrivals(at):
                copy.start()
        for total in totals:
            total[...] = jnp.zeros_like(total)

    def arrived(at):
        for copy in arrivals(at):
            copy.wait()

    for at in range(slabs):
        pl.when(x == at)(functools.partial(arrived, at))

    def add(first, last):
        for total, (low, high, sides) in zip(totals, terms):
            tall = (high - low) * rows
            left = jnp.concatenate(
                [
                    held[
                        low * rows : high * rows,
                        pl.ds(pl.multiple_of((x - a) * lanes, lanes), lanes),
                    ]
                    for a in range(first, last)
                ],
                axis=0,
            )
            right = [fields[f][0, b * size_z : b * size_z + lanes, :] for f, b in sides]
            total[first * tall : last * tall] += jnp.dot(
                left, jnp.concatenate(right, axis=1), preferred_element_type=jnp.float32
            )

    for first, last, chosen in (
        (0, 1, x == 0),
        (0, 2, x == 1),
        (0, 3, jnp.logical_and(x > 1, x < slabs)),
        (1, 3, x == slabs),
        (2, 3, x == slabs + 1),
    ):
        pl.when(chosen)(functools.partial(add, first, last))

    if field_count == 1:
        return

    @pl.when(x == slabs + 1)
    def _():
        late, beside, third = totals
        for i, block in enumerate((0, 1, 2, 3, 6, 7, 4, 5)):
            for n in range(2):
                for a in range(3):
                    for b in range(3):
                        if b == 2:
                            source, at, column = third, a * 8 + i, n
                        elif n == 1:
                            source, at, column = beside, a * 8 + i, b
                        elif i < 6:
                            source, at, column = early, a * 6 + i, b
                        else:
                            source, at, column = late, a * 2 + i - 6, b
                        to = (3 * a + b) * 96
                        out_ref[block, n, :, to : to + 96] = source[
                            at * rows : (at + 1) * rows, column * 128 : column * 128 + 96
                        ]
                out_ref[block, n, :, 864:] = jnp.zeros((rows, 32), jnp.float32)


def product(blocks, fields, early, size_z):
    count = len(blocks)
    rows = blocks[0][0].shape[0]
    shape = fields[0].shape
    slabs = shape[0] - 2
    cells = slabs * (shape[1] - 2 * size_z)
    cuts = tuple(len(parts) for parts in blocks)
    field = pl.BlockSpec((1,) + shape[1:], lambda x: (x, 0, 0))
    whole = pl.BlockSpec((3 * 6 * rows, 256), lambda x: (0, 0))
    in_specs = [pl.BlockSpec(memory_space=pl.ANY)] * sum(cuts) + [field] * len(fields)
    scratch = []
    if early is None:
        terms = ((0, 6, ((0, 0), (0, 1))),)
        out_specs, out_shape = whole, jax.ShapeDtypeStruct((3 * 6 * rows, 256), jnp.float32)
    else:
        terms = ((6, 8, ((0, 0), (0, 1))), (0, 8, ((1, 0), (1, 1))), (0, 8, ((0, 2), (1, 2))))
        in_specs.append(whole)
        out_specs = pl.BlockSpec((count, 2, rows, 896), lambda x: (0, 0, 0, 0))
        out_shape = jax.ShapeDtypeStruct((count, 2, rows, 896), jnp.float32)
        scratch = [pltpu.VMEM((3 * (h - w) * rows, 256), jnp.float32) for w, h, _ in terms]
    return pl.pallas_call(
        functools.partial(product_body, cuts, slabs, size_z, terms, len(fields)),
        grid=(slabs + 2,),
        in_specs=in_specs,
        out_specs=out_specs,
        out_shape=out_shape,
        scratch_shapes=scratch
        + [
            pltpu.VMEM((count * rows, cells), fields[0].dtype),
            pltpu.SemaphoreType.DMA((count, slabs)),
        ],
        compiler_params=pltpu.CompilerParams(vmem_limit_bytes=VMEM),
        cost_estimate=pl.CostEstimate(
            flops=len(terms) * 6 * 10**9, bytes_accessed=16 * 2**20, transcendentals=0
        ),
    )(*[part for parts in blocks for part in parts], *fields, *([] if early is None else [early]))


def ring_sum(piece):
    up, down = piece(4), piece(-3)
    for step in (3, 2, 1):
        up = shift(up, z=1) + piece(step)
        if step > 1:
            down = shift(down, z=-1) + piece(1 - step)
        up, down = lax.optimization_barrier((up, down))
    return shift(up, z=1) + shift(down, z=-1) + piece(0)


def shards(activations, out_grad):
    count, slab_x, size_y, size_z = activations.shape
    lanes = size_y * size_z
    cells = slab_x * lanes
    half = cells // 2
    space, chan = lax.axis_index("space"), lax.axis_index("chan")
    z, high = space % 8, space // 8
    y, x, k = chan // 4, chan // 2 % 2, chan % 2

    def cross(value, bits):
        return send(value, lambda d: dict(d, y=d["y"] ^ bits))

    cut = slab_x // 2
    one = out_grad[:, :cut].reshape(count, half)
    one, out_grad = lax.optimization_barrier((one, out_grad))
    next_one = cross(one, 1)
    two = out_grad[:, cut:].reshape(count, half)
    two, activations = lax.optimization_barrier((two, activations))
    last_two = cross(two, 3)
    next_two, last_one = cross(two, 1), cross(one, 3)
    acts = activations.reshape(count, cells)
    acts_near = send(acts, lambda d: dict(d, x=d["x"] ^ 1))

    def ends(flip):
        def move(value, step):
            pairs = []
            for i in range(256):
                d = place(i)
                space_to = d["h"] * 8 + d["z"] + step
                if 0 <= space_to < 16:
                    to = dict(d, h=space_to // 8, z=space_to % 8, x=d["x"] ^ flip)
                    pairs.append((i, index_of(to)))
            return lax.ppermute(value, AXES, pairs)

        return move(acts[:, cells - lanes :], 1), move(acts[:, :lanes], -1)

    own_ends, near_ends = ends(0), ends(1)
    next_one, last_two, own_ends = lax.optimization_barrier((next_one, last_two, own_ends))
    far_one, far_two = cross(next_one, 3), cross(last_two, 1)
    own = spread(acts, jnp.concatenate(own_ends, axis=1), size_z, lanes)
    next_one, last_two, next_two, last_one, own = lax.optimization_barrier(
        (next_one, last_two, next_two, last_one, own)
    )
    mates = [
        send(v, lambda d: dict(d, k=d["k"] ^ 1))
        for v in (one, two, next_one, last_two, next_two, last_one)
    ]
    blocks = (
        (one, two),
        (mates[0], mates[1]),
        (next_one, next_two),
        (mates[2], mates[4]),
        (last_one, last_two),
        (mates[5], mates[3]),
    )
    early = product(blocks, (own,), None, size_z)
    early, acts_near, near_ends = lax.optimization_barrier((early, acts_near, near_ends))
    near = spread(acts_near, jnp.concatenate(near_ends, axis=1), size_z, lanes)
    far_one, far_two, near = lax.optimization_barrier((far_one, far_two, near))
    far_mate = shift(far_one, k=1), shift(far_two, k=1)
    parts = product(blocks + ((far_one, far_two), far_mate), (own, near), early, size_z)

    def piece(step):
        to = lax.rem(z + step + 8, 8)
        b, j, c = to // 4, to // 2 % 2, to % 2
        at = (0, (b ^ (y % 2)) * 2 + (c ^ k), j ^ x, 0, 0)
        split = parts.reshape((2, 4) + parts.shape[1:])
        return lax.dynamic_slice(split, at, (2, 1, 1) + parts.shape[2:])[:, 0, 0]

    mine = ring_sum(piece)
    here = (high == y // 2).astype(jnp.int32)
    keep = lax.dynamic_index_in_dim(mine, 1 - here, 0, False)
    give = lax.dynamic_index_in_dim(mine, here, 0, False)

    def turned(d, flip):
        bits = d["z"]
        low = bits // 2 % 2
        return dict(d, z=bits + 2 * (d["x"] - low), x=low, h=d["h"] + flip)

    total = send(keep, lambda d: turned(d, 0)) + send(give, lambda d: turned(d, 1))
    scale = jnp.float32(1.0) / jnp.sqrt(jnp.float32(cells * lax.axis_size("space")))
    total = (total[:, : 27 * count] * scale).reshape(count, 27, count)
    return jnp.transpose(total, (1, 0, 2))


def solution(mesh):
    return jax.shard_map(
        shards,
        mesh=mesh,
        in_specs=(P("chan", "space", None, None), P("chan", "space", None, None)),
        out_specs=P(None, "space", "chan"),
        check_vma=False,
    )
```

```python
import functools

import jax
import jax.numpy as jnp
from jax import lax
from jax.experimental import pallas as pl
from jax.experimental.pallas import tpu as pltpu
from jax.sharding import PartitionSpec as P


AXES = ("space", "chan")
VMEM = 52 * 2**20
SIZES = (("h", 2), ("z", 8), ("y", 4), ("x", 2), ("k", 2))


def place(index):
    found = {}
    for name, size in reversed(SIZES):
        index, found[name] = divmod(index, size)
    return found


def index_of(found):
    index = 0
    for name, size in SIZES:
        index = index * size + found[name] % size
    return index


def send(value, move):
    pairs = [(i, index_of(move(place(i)))) for i in range(256)]
    return lax.ppermute(value, AXES, pairs)


def shift(value, **steps):
    return send(value, lambda d: {n: d[n] + steps.get(n, 0) for n in d})


def spread_body(size_z, slabs, lanes, middle, edge, out_ref):
    rows = middle.shape[0]
    z = lax.broadcasted_iota(jnp.int32, (rows, lanes), 1) % size_z
    blank = jnp.zeros((size_z, out_ref.shape[2]), out_ref.dtype)
    for part in range(out_ref.shape[0]):
        x = pl.program_id(0) * out_ref.shape[0] + part
        inside = jnp.logical_and(x > 0, x <= slabs)
        at = pl.multiple_of(jnp.clip(x - 1, 0, slabs - 1) * lanes, lanes)
        side = pl.multiple_of(x // (slabs + 1) * lanes, lanes)
        center = jnp.where(
            inside,
            middle[:, pl.ds(at, lanes)].astype(jnp.float32),
            edge[:, pl.ds(side, lanes)].astype(jnp.float32),
        )
        below = jnp.where(z == 0, 0.0, pltpu.roll(center, 1, 1))
        above = jnp.where(z == size_z - 1, 0.0, pltpu.roll(center, lanes - 1, 1))
        stack = [below, center, above, jnp.zeros((rows, lanes), jnp.float32)]
        turned = jnp.concatenate(stack, axis=0).T.astype(out_ref.dtype)
        out_ref[part, :size_z] = blank
        out_ref[part, size_z : size_z + lanes] = turned
        out_ref[part, size_z + lanes :] = blank


def spread(cells, edges, size_z, lanes):
    rows, total = cells.shape
    slabs = total // lanes
    shape = (slabs + 2, lanes + 2 * size_z, 4 * rows)
    return pl.pallas_call(
        functools.partial(spread_body, size_z, slabs, lanes),
        grid=((slabs + 2) // 2,),
        in_specs=[
            pl.BlockSpec(cells.shape, lambda x: (0, 0)),
            pl.BlockSpec(edges.shape, lambda x: (0, 0)),
        ],
        out_specs=pl.BlockSpec((2,) + shape[1:], lambda x: (x, 0, 0)),
        out_shape=jax.ShapeDtypeStruct(shape, cells.dtype),
        compiler_params=pltpu.CompilerParams(vmem_limit_bytes=VMEM),
        cost_estimate=pl.CostEstimate(
            flops=10 * 2**20, bytes_accessed=10 * 2**20, transcendentals=0
        ),
    )(cells, edges)


def product_body(cuts, slabs, size_z, *refs):
    count = len(cuts)
    refs = list(refs)
    blocks = [[refs.pop(0) for _ in range(cut)] for cut in cuts]
    own, near, out_ref, held, total, sems = refs
    x = pl.program_id(0)
    lanes = held.shape[1] // slabs
    rows = held.shape[0] // count
    tall = count * rows

    def arrivals(at):
        copies = []
        for i, parts in enumerate(blocks):
            part, inner = divmod(at, slabs // len(parts))
            copies.append(
                pltpu.make_async_copy(
                    parts[part].at[:, pl.ds(inner * lanes, lanes)],
                    held.at[pl.ds(i * rows, rows), pl.ds(at * lanes, lanes)],
                    sems.at[i, at],
                )
            )
        return copies

    @pl.when(x == 0)
    def _():
        for at in range(slabs):
            for copy in arrivals(at):
                copy.start()
        total[...] = jnp.zeros_like(total)

    def arrived(at):
        for copy in arrivals(at):
            copy.wait()

    for at in range(slabs):
        pl.when(x == at)(functools.partial(arrived, at))

    def add(first, last):
        left = jnp.concatenate(
            [
                held[:, pl.ds(pl.multiple_of((x - a) * lanes, lanes), lanes)]
                for a in range(first, last)
            ],
            axis=0,
        )
        for b in range(3):
            at = slice(b * size_z, b * size_z + lanes)
            total[b, first * tall : last * tall] += jnp.dot(
                left,
                jnp.concatenate([own[0, at, :], near[0, at, :]], axis=1),
                preferred_element_type=jnp.float32,
            )

    for first, last, chosen in (
        (0, 1, x == 0),
        (0, 2, x == 1),
        (0, 3, jnp.logical_and(x > 1, x < slabs)),
        (1, 3, x == slabs),
        (2, 3, x == slabs + 1),
    ):
        pl.when(chosen)(functools.partial(add, first, last))

    @pl.when(x == slabs + 1)
    def _():
        for block in range(count):
            for n in range(2):
                for a in range(3):
                    for b in range(3):
                        at = a * tall + block * rows
                        to = (3 * a + b) * 96
                        out_ref[block, n, :, to : to + 96] = total[
                            b, at : at + rows, n * 128 : n * 128 + 96
                        ]
                out_ref[block, n, :, 864:] = jnp.zeros((rows, 32), jnp.float32)


def product(blocks, own, near, size_z):
    count = len(blocks)
    rows = blocks[0][0].shape[0]
    slabs = own.shape[0] - 2
    cells = slabs * (own.shape[1] - 2 * size_z)
    cuts = tuple(len(parts) for parts in blocks)
    field = pl.BlockSpec((1,) + own.shape[1:], lambda x: (x, 0, 0))
    return pl.pallas_call(
        functools.partial(product_body, cuts, slabs, size_z),
        grid=(slabs + 2,),
        in_specs=[pl.BlockSpec(memory_space=pl.ANY)] * sum(cuts) + [field, field],
        out_specs=pl.BlockSpec((count, 2, rows, 896), lambda x: (0, 0, 0, 0)),
        out_shape=jax.ShapeDtypeStruct((count, 2, rows, 896), jnp.float32),
        scratch_shapes=[
            pltpu.VMEM((count * rows, cells), own.dtype),
            pltpu.VMEM((3, 3 * count * rows, 2 * own.shape[2]), jnp.float32),
            pltpu.SemaphoreType.DMA((count, slabs)),
        ],
        compiler_params=pltpu.CompilerParams(vmem_limit_bytes=VMEM),
        cost_estimate=pl.CostEstimate(
            flops=count * 3 * 10**9, bytes_accessed=16 * 2**20, transcendentals=0
        ),
    )(*[part for parts in blocks for part in parts], own, near)


def ring_sum(piece):
    up, down = piece(4), piece(-3)
    for step in (3, 2, 1):
        up = shift(up, z=1) + piece(step)
        if step > 1:
            down = shift(down, z=-1) + piece(1 - step)
    return shift(up, z=1) + shift(down, z=-1) + piece(0)


def shards(activations, out_grad):
    count, slab_x, size_y, size_z = activations.shape
    lanes = size_y * size_z
    cells = slab_x * lanes
    half = cells // 2
    space, chan = lax.axis_index("space"), lax.axis_index("chan")
    z, high = space % 8, space // 8
    y, x, k = chan // 4, chan // 2 % 2, chan % 2

    def cross(value, bits):
        return send(value, lambda d: dict(d, y=d["y"] ^ bits))

    cut = slab_x // 2
    one = out_grad[:, :cut].reshape(count, half)
    one, out_grad = lax.optimization_barrier((one, out_grad))
    next_one = cross(one, 1)
    two = out_grad[:, cut:].reshape(count, half)
    two, activations = lax.optimization_barrier((two, activations))
    last_two = cross(two, 3)
    next_two, last_one = cross(two, 1), cross(one, 3)
    acts = activations.reshape(count, cells)
    acts_near = send(acts, lambda d: dict(d, x=d["x"] ^ 1))

    def ends(flip):
        def move(value, step):
            pairs = []
            for i in range(256):
                d = place(i)
                space_to = d["h"] * 8 + d["z"] + step
                if 0 <= space_to < 16:
                    to = dict(d, h=space_to // 8, z=space_to % 8, x=d["x"] ^ flip)
                    pairs.append((i, index_of(to)))
            return lax.ppermute(value, AXES, pairs)

        return move(acts[:, cells - lanes :], 1), move(acts[:, :lanes], -1)

    own_ends, near_ends = ends(0), ends(1)
    next_one, last_two, own_ends = lax.optimization_barrier((next_one, last_two, own_ends))
    far_one, far_two = cross(next_one, 3), cross(last_two, 1)
    own = spread(acts, jnp.concatenate(own_ends, axis=1), size_z, lanes)
    next_one, last_two, next_two, last_one, own = lax.optimization_barrier(
        (next_one, last_two, next_two, last_one, own)
    )
    mates = [shift(v, k=1) for v in (one, two, next_one, last_two, next_two, last_one)]
    near = spread(acts_near, jnp.concatenate(near_ends, axis=1), size_z, lanes)
    far_one, far_two, near, mates = lax.optimization_barrier((far_one, far_two, near, mates))
    far_mate = shift(far_one, k=1), shift(far_two, k=1)
    blocks = (
        (one, two),
        (mates[0], mates[1]),
        (next_one, next_two),
        (mates[2], mates[4]),
        (far_one, far_two),
        far_mate,
        (last_one, last_two),
        (mates[5], mates[3]),
    )
    parts = product(blocks, own, near, size_z)

    def piece(step):
        to = lax.rem(z + step + 8, 8)
        b, j, c = to // 4, to // 2 % 2, to % 2
        at = (0, (b ^ (y % 2)) * 2 + (c ^ k), j ^ x, 0, 0)
        split = parts.reshape((2, 4) + parts.shape[1:])
        return lax.dynamic_slice(split, at, (2, 1, 1) + parts.shape[2:])[:, 0, 0]

    mine = ring_sum(piece)
    here = (high == y // 2).astype(jnp.int32)
    keep = lax.dynamic_index_in_dim(mine, 1 - here, 0, False)
    give = lax.dynamic_index_in_dim(mine, here, 0, False)

    def turned(d, flip):
        bits = d["z"]
        low = bits // 2 % 2
        return dict(d, z=bits + 2 * (d["x"] - low), x=low, h=d["h"] + flip)

    total = send(keep, lambda d: turned(d, 0)) + send(give, lambda d: turned(d, 1))
    scale = jnp.float32(1.0) / jnp.sqrt(jnp.float32(cells * lax.axis_size("space")))
    total = (total[:, : 27 * count] * scale).reshape(count, 27, count)
    return jnp.transpose(total, (1, 0, 2))


def solution(mesh):
    return jax.shard_map(
        shards,
        mesh=mesh,
        in_specs=(P("chan", "space", None, None), P("chan", "space", None, None)),
        out_specs=P(None, "space", "chan"),
        check_vma=False,
    )
```
